512 devices in a mesh: lat: 16 (over y, core), wave: 32 (over z, x).
Axes of the slice: x: 4, y: 8, z: 8, core: 2. Of those that a mesh axis runs over, the one named last changes fastest.
Arguments:
- fourier: bfloat16 [1024, 12, 1280], P(('lat', 'wave')), may hold values from -6 to 6
- wave_table: int32 [1280], replicated, may hold values from 0 to 1279, each once
- legendre: bfloat16 [1280, 512, 1280], P('wave', 'lat'), may hold values from -0.25 to 0.25
Outputs:
- spectral: float32 [1280, 12, 1280], P('wave', None, 'lat')
The draws below stay inside these ranges and needn't reach their ends.
Inputs may be any that keep to these rules, and one draw needn't show every extreme that they name: `wave_table`: every wavenumber 0 to 1279 stands in exactly one slot.
All inputs are finite; a program needn't handle non-finite values.
Results may differ from the reference program's by a relative error of at most 0.0031.
Values may be sent and summed in bfloat16 or wider, within the bound.
A program may use at most 128 MiB of HBM per device.

```python
import jax
import jax.numpy as jnp
from jax import lax

M = 1280
N = 1280
PD = 32
COLS = 12
BANDS = 16
PAIRS = 512
ROWS = 1024


def raised(values, stream_key, source, target, shards_of, factor):
    def block_of(axis_at):
        return (jnp.arange(values.shape[axis_at]) // (values.shape[axis_at] // shards_of)).reshape((-1,) + (1,) * (values.ndim - 1 - axis_at))

    one_side = jax.random.permutation(stream_key, shards_of)[block_of(target)]
    second = (block_of(target) + shards_of // 2) % shards_of
    return jnp.where((block_of(source) == one_side) | (block_of(source) == second), factor * values, values)


def steps_of(rng, shape, pieces, low, high):
    def one(position, shards_of):
        heights = jax.random.uniform(jax.random.fold_in(jax.random.fold_in(rng, 6), position), (shards_of,), jnp.float32, low / len(pieces), high / len(pieces))
        return jnp.repeat(jnp.exp(heights), shape[position] // shards_of).reshape((-1,) + (1,) * (len(shape) - position - 1))

    gain = one(*pieces[0])
    for cut in pieces[1:]:
        gain = gain * one(*cut)
    return gain


def gaussian(key, dims, width, most, split=(), held_as=jnp.bfloat16):
    level = steps_of(key, dims, split, -0.22, 0.18) if split else 1.0
    values = jax.random.normal(key, dims, jnp.float32) * width * level
    return jnp.minimum(jnp.maximum(values, -most), most).astype(held_as)


def heavy_noise(rng, extent, spread, limit, shards, heavy, kind=jnp.bfloat16):
    entries = spread * jax.random.normal(rng, extent, jnp.float32)
    if shards:
        entries = entries * steps_of(rng, extent, shards, -0.22, 0.18)
    return jnp.clip(raised(entries, jax.random.fold_in(rng, 3), *heavy), -limit, limit).astype(kind)


def setup_inputs(seed: int = 0) -> dict:
    keys = jax.random.split(jax.random.key(seed), 4)
    return {
        "fourier": gaussian(keys[0], (ROWS, COLS, M), 1.0, 6.0, ((0, 512),)),
        "wave_table": jax.random.permutation(keys[1], M).astype(jnp.int32),
        "legendre": heavy_noise(keys[2], (M, PAIRS, N), (2 * PAIRS) ** -0.5, 0.25, ((0, 32), (1, 16)), (1, 2, 16, 2.0)),
    }


def reference(fourier, wave_table, legendre):
    handled = jnp.arange(PAIRS, dtype=jnp.int32)
    band_block = handled // PD
    band_offset = handled % PD
    pair_index = jnp.where(band_block < BANDS // 2, 2 * PD * band_block + band_offset, 2 * PD * (BANDS - 1 - band_block) + PD + band_offset)
    south_index = ROWS - 1 - pair_index
    half_degrees = N // 2
    degree_slot = jnp.arange(N, dtype=jnp.int32)
    offsets = jnp.where(degree_slot < half_degrees, 2 * degree_slot, 2 * (degree_slot - half_degrees) + 1)

    def per_wave(inputs):
        wave_number, table = inputs
        wave_rows = lax.dynamic_index_in_dim(fourier, wave_number, 2, keepdims=False)
        north_rows = wave_rows[pair_index].astype(jnp.float32)
        south_rows = wave_rows[south_index].astype(jnp.float32)
        even_part = (north_rows + south_rows).astype(jnp.bfloat16)
        odd_part = (north_rows - south_rows).astype(jnp.bfloat16)
        even_out = jnp.dot(even_part.T, table[:, :half_degrees], preferred_element_type=jnp.float32)
        odd_out = jnp.dot(odd_part.T, table[:, half_degrees:], preferred_element_type=jnp.float32)
        result = jnp.concatenate([even_out, odd_out], axis=1)
        inside = offsets[None, :] < (N - wave_number)
        return jnp.where(inside, result, jnp.zeros_like(result))

    return lax.map(per_wave, (wave_table, legendre))
```

```python
import functools

import jax
import jax.numpy as jnp
from jax import lax
from jax.experimental import pallas as pl
from jax.experimental.pallas import tpu as pltpu
from jax.sharding import PartitionSpec as P

MESH = pl.DeviceIdType.MESH
F32, BF16, I32 = jnp.float32, jnp.bfloat16, jnp.int32

LATS, WAVES, CHIPS = 16, 32, 8
SLOTS, COLS, PAIRS, DEG = 40, 12, 32, 1280
OWN = 80
ROWS = 304
GROUPS = 5
PIECES = ((0, 304),)


def lanes(shape):
    return lax.broadcasted_iota(I32, shape, len(shape) - 1)


def kernel(fo_hbm, wt_hbm, leg_hbm, out_ref, fo, wt, leg, vg, snd, ns, eo, lhs, lim,
           part, sib, rsnd, rrcv, in_sem, a_send, a_recv, s_send, s_recv, r_send, r_recv):
    lat = lax.axis_index("lat")
    wave = lax.axis_index("wave")
    chip, core = lat // 2, lat % 2
    step = 1 - 2 * core
    mirror = LATS - 1 - lat
    half = wave // 16
    target_lat = jnp.where(half == 1, mirror, lat)

    def chip_at(distance):
        return (chip + distance * step + 2 * CHIPS) % CHIPS

    up = chip_at(1)

    load_fo = pltpu.make_async_copy(fo_hbm, fo, in_sem.at[0])
    load_wt = pltpu.make_async_copy(wt_hbm, wt, in_sem.at[1])
    load_leg = pltpu.make_async_copy(leg_hbm, leg, in_sem.at[2])
    load_fo.start()
    load_wt.start()
    load_leg.start()

    barrier = pltpu.get_barrier_semaphore()

    def greet(d, carry):
        other = (wave + d) % WAVES
        at = jnp.where(other < 16, lat, mirror)
        pl.semaphore_signal(barrier, inc=1, device_id=(at, other), device_id_type=MESH)
        return carry

    lax.fori_loop(1, WAVES, greet, 0)

    @pl.when(half == 1)
    def _():
        pl.semaphore_signal(barrier, inc=1, device_id=(mirror, wave), device_id_type=MESH)

    pl.semaphore_signal(barrier, inc=1, device_id=(lat + step, wave), device_id_type=MESH)
    below, above = (chip + CHIPS - 1) % CHIPS, (chip + 1) % CHIPS
    pl.semaphore_signal(barrier, inc=1, device_id=(2 * below, wave), device_id_type=MESH)
    pl.semaphore_signal(barrier, inc=1, device_id=(2 * above + 1, wave), device_id_type=MESH)

    load_fo.wait()
    load_wt.wait()
    south = lat >= LATS // 2
    first, second = fo[0].astype(F32), fo[1].astype(F32)
    row_a = jnp.where(south, second, first)
    row_b = jnp.where(south, first, second)
    for g in range(3):
        vg[g] = jnp.concatenate([row_a[4 * g:4 * g + 4], row_b[4 * g:4 * g + 4]], axis=0)
    lane8 = lanes((8, 128))

    def table_lanes(start):
        row, off = start // 128, start % 128
        back = (128 - off) % 128
        near = jnp.broadcast_to(wt[pl.ds(row, 1), :], (8, 128))
        far = jnp.broadcast_to(wt[pl.ds(jnp.minimum(row + 1, 9), 1), :], (8, 128))
        return jnp.where(lane8 < 128 - off, pltpu.roll(near, back, 1), pltpu.roll(far, back, 1))

    def pick(t, carry):
        index = table_lanes(120 * t)
        low, high = index & 127, index >> 7
        found = []
        for g in range(3):
            acc = jnp.zeros((8, 128), F32)
            for u in range(10):
                got = jnp.take_along_axis(vg[g, :, 128 * u:128 * u + 128], low, axis=1,
                                          mode="promise_in_bounds")
                acc = jnp.where(high == u, got, acc)
            found.append(acc)
        for d in range(3):
            turned = [found[g] if g == d else pltpu.roll(found[g], (40 * (g - d)) % 128, 1)
                      for g in range(3)]
            message = jnp.where(lane8 < 40, turned[0], jnp.where(lane8 < 80, turned[1], turned[2]))
            snd[3 * t + d] = message.astype(BF16)
        return carry

    lax.fori_loop(0, 11, pick, 0)

    mine = jnp.broadcast_to(table_lanes(SLOTS * wave)[0:1].astype(F32), (128, 128))
    lim[...] = DEG - mine.T[:SLOTS]

    pl.semaphore_wait(barrier, 34 + half)

    place = jnp.where(south, 16 + 15 - wave % 16, wave % 16)

    def exchange(d):
        to = (wave + d) % WAVES
        return pltpu.make_async_remote_copy(
            src_ref=snd.at[to], dst_ref=ns.at[place], send_sem=a_send.at[d],
            recv_sem=a_recv.at[place], device_id=(target_lat, to), device_id_type=MESH)

    def start_exchange(d, carry):
        exchange(d).start()
        return carry

    lax.fori_loop(1, WAVES, start_exchange, 0)
    stay = pltpu.make_async_copy(snd.at[wave], ns.at[place], a_recv.at[place])

    @pl.when(half == 1)
    def _():
        exchange(0).start()

    @pl.when(half == 0)
    def _():
        stay.start()

    load_leg.wait()

    def arrive(s, carry):
        pltpu.make_async_copy(snd.at[0], ns.at[s], a_recv.at[s]).wait()
        return carry

    lax.fori_loop(0, WAVES, arrive, 0)

    north = ns[0:16].astype(F32)
    southern = ns[16:32].astype(F32)
    eo[0] = (north + southern).astype(BF16).astype(F32).reshape(128, 128)
    eo[1] = (north - southern).astype(BF16).astype(F32).reshape(128, 128)
    sub = lax.broadcasted_iota(I32, (8, 128), 0)
    keep = [sub == 4 * kt + lane8 // 32 for kt in range(2)]
    for part_of in range(2):
        for pair in range(2):
            turned = []
            for c4 in (2 * pair, 2 * pair + 1):
                x = eo[part_of, pl.ds(c4, 32, stride=4), :]
                turned.append(jnp.concatenate([x] * 4, axis=0).T)
            for g in range(3):
                c = 4 * g + 2 * pair
                for q in range(GROUPS):
                    at = 40 * g + 8 * q
                    for kt in range(2):
                        both = jnp.concatenate(
                            [jnp.where(keep[kt], t[at:at + 8], 0.0) for t in turned], axis=0)
                        lhs[part_of, q, 8 * c:8 * c + 16, 128 * kt:128 * kt + 128] = both.astype(BF16)

    lane96 = lanes((96, 128))

    def product(job, owner):
        off = 32 * (owner % 4)
        column = pl.multiple_of(128 * ((5 * owner) // 4), 128)
        placed = [[], []]
        for q in range(GROUPS):
            right = leg[8 * q:8 * q + 8, :, pl.ds(column, 256)].reshape(256, 256)
            got = jnp.dot(lhs[owner // 4, q], right, preferred_element_type=F32)
            for e in range(2):
                start = off + OWN * e
                window = jnp.where(lane96 >= start, got[:, :128], got[:, 128:])
                placed[e].append(pltpu.roll(window, (OWN * q + 256 - start) % 128, 1))
        for e in range(2):
            z = placed[e]
            part[job, e, 0:96] = jnp.where(lane96 < 80, z[0], z[1])
            part[job, e, 96:192] = jnp.where(lane96 < 32, z[1], jnp.where(lane96 < 112, z[2], z[3]))
            part[job, e, 192:288] = jnp.where(lane96 < 64, z[3], z[4])
            for v, count in ((0, 8), (1, 4)):
                rest = z[4][64 * v:64 * v + 8]
                for n in range(1, count):
                    c = 8 * v + n
                    rest = jnp.where(lane8 // 16 == n, pltpu.roll(z[4][8 * c:8 * c + 8], 16 * n, 1), rest)
                part[job, e, 288 + 8 * v:296 + 8 * v] = rest

    def to_sibling(job, e, slot):
        return pltpu.make_async_remote_copy(
            src_ref=part.at[job, e], dst_ref=sib.at[slot], send_sem=s_send.at[slot],
            recv_sem=s_recv.at[slot], device_id=(lat + step, wave), device_id_type=MESH)

    def ring(slot, piece, at_lat, to_slot):
        low, high = PIECES[piece]
        return pltpu.make_async_remote_copy(
            src_ref=rsnd.at[slot, low:high], dst_ref=rrcv.at[to_slot, low:high],
            send_sem=r_send.at[slot, piece], recv_sem=r_recv.at[to_slot, piece],
            device_id=(at_lat, wave), device_id_type=MESH)

    same = 2 * up + core

    def pass_on(slot, job, e, from_sib, arrived, at_lat, to_slot):
        for piece, (low, high) in enumerate(PIECES):
            total = part[job, e, low:high] + sib[from_sib, low:high]
            if arrived is not None:
                ring(0, piece, same, arrived).wait_recv()
                total = total + rrcv[arrived, low:high].astype(F32)
            rsnd[slot, low:high] = total.astype(BF16)
            ring(slot, piece, at_lat, to_slot).start()

    other = 1 - core

    def work(job, carry):
        toward = job % 2 == 0
        far = jnp.where(job == 0, 4, jnp.where(job == 7, 0, 3 - (job - 1) // 2))
        owner = chip_at(jnp.where(toward, far, -far))
        product(job, owner)

        @pl.when(job == 0)
        def _():
            to_sibling(0, other, 0).start()

        for k in (1, 3, 5):
            @pl.when(job == k)
            def _():
                to_sibling(k, 0, k).start()
                to_sibling(k, 1, k + 1).start()

        @pl.when(job == 7)
        def _():
            to_sibling(7, other, 7).start()

        @pl.when(job == 1)
        def _():
            to_sibling(0, other, 0).wait_recv()
            pass_on(0, 0, core, 0, None, same, 0)

        @pl.when(job == 2)
        def _():
            to_sibling(1, 0, 1).wait_recv()
            to_sibling(1, 1, 2).wait_recv()
            pass_on(1 + other, 2, other, 1 + other, None, same, 1 + other)

        @pl.when(job == 3)
        def _():
            pass_on(1 + core, 2, core, 1 + core, 0, same, 1 + core)

        @pl.when(job == 4)
        def _():
            to_sibling(3, 0, 3).wait_recv()
            to_sibling(3, 1, 4).wait_recv()
            pass_on(3 + other, 4, other, 3 + other, 1 + other, same, 3 + other)

        @pl.when(job == 5)
        def _():
            pass_on(3 + core, 4, core, 3 + core, 1 + core, same, 3 + core)

        @pl.when(job == 6)
        def _():
            to_sibling(5, 0, 5).wait_recv()
            to_sibling(5, 1, 6).wait_recv()
            pass_on(5 + other, 6, other, 5 + other, 3 + other, 2 * up + other, 5 + core)

        @pl.when(job == 7)
        def _():
            pass_on(5 + core, 6, core, 5 + core, 3 + core, 2 * up + core, 5 + core)

        return carry

    lax.fori_loop(0, 8, work, 0)

    to_sibling(7, other, 7).wait_recv()
    for slot in (5, 6):
        for piece in range(len(PIECES)):
            ring(0, piece, same, slot).wait_recv()

    def total(low, high):
        return (part[7, core, low:high] + sib[7, low:high]
                + rrcv[5, low:high].astype(F32) + rrcv[6, low:high].astype(F32))

    t0, t1, t2, rest = total(0, 96), total(96, 192), total(192, 288), total(288, 304)
    spread = jnp.concatenate(
        [rest[8 * (c // 8):8 * (c // 8) + 8] if c % 8 == 0
         else pltpu.roll(rest[8 * (c // 8):8 * (c // 8) + 8], 128 - 16 * (c % 8), 1)
         for c in range(COLS)], axis=0)
    z = [t0,
         pltpu.roll(jnp.where(lane96 >= 80, t0, t1), 48, 1),
         pltpu.roll(t1, 96, 1),
         pltpu.roll(jnp.where(lane96 >= 112, t1, t2), 16, 1),
         pltpu.roll(jnp.where(lane96 >= 64, t2, spread), 64, 1)]
    degree = OWN * lat + lane8
    offset = jnp.where(degree < DEG // 2, 2 * degree, 2 * degree - (DEG - 1)).astype(F32)
    for q in range(GROUPS):
        inside = offset < lim[8 * q:8 * q + 8]
        for c in range(COLS):
            value = jnp.where(inside, z[q][8 * c:8 * c + 8], 0.0)
            out_ref[c, 8 * q:8 * q + 8, :] = value[:, :OWN]

    def sent(d, carry):
        exchange(d).wait_send()
        return carry

    lax.fori_loop(1, WAVES, sent, 0)

    @pl.when(half == 1)
    def _():
        exchange(0).wait_send()

    for slot in range(8):
        to_sibling(0, 0, slot).wait_send()
    for slot in range(7):
        for piece in range(len(PIECES)):
            ring(slot, piece, same, 0).wait_send()


def local(fourier, wave_table, legendre):
    table = wave_table.reshape(10, 128)
    hbm = pl.BlockSpec(memory_space=pltpu.MemorySpace.HBM)
    out = pl.pallas_call(
        kernel,
        out_shape=jax.ShapeDtypeStruct((COLS, SLOTS, OWN), F32),
        in_specs=[hbm, hbm, hbm],
        out_specs=pl.BlockSpec(memory_space=pltpu.VMEM),
        scratch_shapes=[
            pltpu.VMEM((2, COLS, DEG), BF16),
            pltpu.VMEM((10, 128), I32),
            pltpu.VMEM((SLOTS, PAIRS, DEG), BF16),
            pltpu.VMEM((3, 8, DEG), F32),
            pltpu.VMEM((33, 8, 128), BF16),
            pltpu.VMEM((32, 8, 128), BF16),
            pltpu.VMEM((2, 128, 128), F32),
            pltpu.VMEM((2, GROUPS, 96, 256), BF16),
            pltpu.VMEM((SLOTS, 128), F32),
            pltpu.VMEM((8, 2, ROWS, 128), F32),
            pltpu.VMEM((8, ROWS, 128), F32),
            pltpu.VMEM((7, ROWS, 128), BF16),
            pltpu.VMEM((7, ROWS, 128), BF16),
            pltpu.SemaphoreType.DMA((3,)),
            pltpu.SemaphoreType.DMA((WAVES,)),
            pltpu.SemaphoreType.DMA((WAVES,)),
            pltpu.SemaphoreType.DMA((8,)),
            pltpu.SemaphoreType.DMA((8,)),
            pltpu.SemaphoreType.DMA((7, len(PIECES))),
            pltpu.SemaphoreType.DMA((7, len(PIECES))),
        ],
        compiler_params=pltpu.CompilerParams(
            collective_id=0, has_side_effects=True, vmem_limit_bytes=48 << 20),
        name="legendre",
    )(fourier, table, legendre)
    return jnp.transpose(out, (1, 0, 2))


def solution(mesh):
    in_specs = (P(("lat", "wave"), None, None), P(), P("wave", "lat", None))
    out_specs = P("wave", None, "lat")
    return jax.shard_map(local, mesh=mesh, in_specs=in_specs, out_specs=out_specs, check_vma=False)
```

```python
import jax
import jax.numpy as jnp
from jax import lax
from jax.experimental import pallas as pl
from jax.experimental.pallas import tpu as pltpu
from jax.sharding import PartitionSpec as P

MESH = pl.DeviceIdType.MESH
F32, BF16, I32 = jnp.float32, jnp.bfloat16, jnp.int32

LATS, WAVES, CHIPS = 16, 32, 8
SLOTS, COLS, PAIRS, DEG = 40, 12, 32, 1280
OWN = 80
ROWS = 304
GROUPS = 5
PIECES = ((0, 160), (160, 304))


def lanes(shape):
    return lax.broadcasted_iota(I32, shape, len(shape) - 1)


def kernel(fo_hbm, wt_hbm, leg_hbm, out_ref, fo, wt, leg, vg, snd, ns, eo, lhs, lim,
           part, sib, rsnd, rrcv, in_sem, a_send, a_recv, s_send, s_recv, r_send, r_recv):
    lat = lax.axis_index("lat")
    wave = lax.axis_index("wave")
    chip, core = lat // 2, lat % 2
    step = 1 - 2 * core
    mirror = LATS - 1 - lat
    half = wave // 16
    target_lat = jnp.where(half == 1, mirror, lat)

    def chip_at(distance):
        return (chip + distance * step + 2 * CHIPS) % CHIPS

    up = chip_at(1)

    load_fo = pltpu.make_async_copy(fo_hbm, fo, in_sem.at[0])
    load_wt = pltpu.make_async_copy(wt_hbm, wt, in_sem.at[1])
    load_leg = pltpu.make_async_copy(leg_hbm, leg, in_sem.at[2])
    load_fo.start()
    load_wt.start()
    load_leg.start()

    barrier = pltpu.get_barrier_semaphore()

    def greet(d, carry):
        other = (wave + d) % WAVES
        at = jnp.where(other < 16, lat, mirror)
        pl.semaphore_signal(barrier, inc=1, device_id=(at, other), device_id_type=MESH)
        return carry

    lax.fori_loop(1, WAVES, greet, 0)

    @pl.when(half == 1)
    def _():
        pl.semaphore_signal(barrier, inc=1, device_id=(mirror, wave), device_id_type=MESH)

    pl.semaphore_signal(barrier, inc=1, device_id=(lat + step, wave), device_id_type=MESH)
    for away in (1, 2):
        for way in range(2):
            back = (chip + CHIPS - away * (1 - 2 * way)) % CHIPS
            pl.semaphore_signal(barrier, inc=1, device_id=(2 * back + way, wave), device_id_type=MESH)

    load_fo.wait()
    load_wt.wait()
    south = lat >= LATS // 2
    rows = fo[...].astype(F32)
    first, second = rows[:, 0, :], rows[:, 1, :]
    row_a = jnp.where(south, second, first)
    row_b = jnp.where(south, first, second)
    for g in range(3):
        vg[g] = jnp.concatenate([row_a[4 * g:4 * g + 4], row_b[4 * g:4 * g + 4]], axis=0)
    lane8 = lanes((8, 128))

    def table_lanes(start):
        row, off = start // 128, start % 128
        back = (128 - off) % 128
        near = jnp.broadcast_to(wt[pl.ds(row, 1), :], (8, 128))
        far = jnp.broadcast_to(wt[pl.ds(jnp.minimum(row + 1, 9), 1), :], (8, 128))
        return jnp.where(lane8 < 128 - off, pltpu.roll(near, back, 1), pltpu.roll(far, back, 1))

    def pick(t, carry):
        index = table_lanes(120 * t)
        low, high = index & 127, index >> 7
        found = []
        for g in range(3):
            acc = jnp.zeros((8, 128), F32)
            for u in range(10):
                got = jnp.take_along_axis(vg[g, :, 128 * u:128 * u + 128], low, axis=1,
                                          mode="promise_in_bounds")
                acc = jnp.where(high == u, got, acc)
            found.append(acc)
        for d in range(3):
            turned = [found[g] if g == d else pltpu.roll(found[g], (40 * (g - d)) % 128, 1)
                      for g in range(3)]
            message = jnp.where(lane8 < 40, turned[0], jnp.where(lane8 < 80, turned[1], turned[2]))
            snd[3 * t + d] = message.astype(BF16)
        return carry

    lax.fori_loop(0, 11, pick, 0)

    mine = jnp.broadcast_to(table_lanes(SLOTS * wave)[0:1].astype(F32), (128, 128))
    lim[...] = DEG - mine.T[:SLOTS]

    pl.semaphore_wait(barrier, 36 + half)

    place = jnp.where(south, 16 + 15 - wave % 16, wave % 16)

    def exchange(d):
        kz, kx = d // 4, d % 4
        dz = 4 + ((kz + 1) // 2) * (2 * (kz % 2) - 1) + 8
        dx = 2 + ((kx + 1) // 2) * (2 * (kx % 2) - 1) + 4
        to = 4 * ((wave // 4 + dz) % 8) + (wave + dx) % 4
        return pltpu.make_async_remote_copy(
            src_ref=snd.at[to], dst_ref=ns.at[place], send_sem=a_send.at[d],
            recv_sem=a_recv.at[place], device_id=(target_lat, to), device_id_type=MESH)

    def start_exchange(d, carry):
        exchange(d).start()
        return carry

    lax.fori_loop(0, WAVES - 1, start_exchange, 0)
    stay = pltpu.make_async_copy(snd.at[wave], ns.at[place], a_recv.at[place])

    @pl.when(half == 1)
    def _():
        exchange(WAVES - 1).start()

    @pl.when(half == 0)
    def _():
        stay.start()

    load_leg.wait()

    def arrive(s, carry):
        pltpu.make_async_copy(snd.at[0], ns.at[s], a_recv.at[s]).wait()
        return carry

    lax.fori_loop(0, WAVES, arrive, 0)

    north = ns[0:16].astype(F32)
    southern = ns[16:32].astype(F32)
    eo[0] = (north + southern).astype(BF16).astype(F32).reshape(128, 128)
    eo[1] = (north - southern).astype(BF16).astype(F32).reshape(128, 128)
    sub = lax.broadcasted_iota(I32, (8, 128), 0)
    keep = [sub == 4 * kt + lane8 // 32 for kt in range(2)]
    for part_of in range(2):
        for pair in range(2):
            turned = []
            for c4 in (2 * pair, 2 * pair + 1):
                x = eo[part_of, pl.ds(c4, 32, stride=4), :]
                turned.append(jnp.concatenate([x] * 4, axis=0).T)
            for g in range(3):
                c = 4 * g + 2 * pair
                for q in range(GROUPS):
                    at = 40 * g + 8 * q
                    for kt in range(2):
                        both = jnp.concatenate(
                            [jnp.where(keep[kt], t[at:at + 8], 0.0) for t in turned], axis=0)
                        lhs[part_of, q, 8 * c:8 * c + 16, 128 * kt:128 * kt + 128] = both.astype(BF16)

    lane96 = lanes((96, 128))

    def product(job, owner):
        off = 32 * (owner % 4)
        column = pl.multiple_of(128 * ((5 * owner) // 4), 128)
        placed = [[], []]
        for q in range(GROUPS):
            right = leg[8 * q:8 * q + 8, :, pl.ds(column, 256)].reshape(256, 256)
            got = jnp.dot(lhs[owner // 4, q], right, preferred_element_type=F32)
            for e in range(2):
                start = off + OWN * e
                window = jnp.where(lane96 >= start, got[:, :128], got[:, 128:])
                placed[e].append(pltpu.roll(window, (OWN * q + 256 - start) % 128, 1))
        for e in range(2):
            z = placed[e]
            part[job, e, 0:96] = jnp.where(lane96 < 80, z[0], z[1])
            part[job, e, 96:192] = jnp.where(lane96 < 32, z[1], jnp.where(lane96 < 112, z[2], z[3]))
            part[job, e, 192:288] = jnp.where(lane96 < 64, z[3], z[4])
            for v, count in ((0, 8), (1, 4)):
                rest = z[4][64 * v:64 * v + 8]
                for n in range(1, count):
                    c = 8 * v + n
                    rest = jnp.where(lane8 // 16 == n, pltpu.roll(z[4][8 * c:8 * c + 8], 16 * n, 1), rest)
                part[job, e, 288 + 8 * v:296 + 8 * v] = rest

    def to_sibling(job, e, slot):
        return pltpu.make_async_remote_copy(
            src_ref=part.at[job, e], dst_ref=sib.at[slot], send_sem=s_send.at[slot],
            recv_sem=s_recv.at[slot], device_id=(lat + step, wave), device_id_type=MESH)

    def ring(slot, piece, at_lat, to_slot):
        low, high = PIECES[piece]
        return pltpu.make_async_remote_copy(
            src_ref=rsnd.at[slot, low:high], dst_ref=rrcv.at[to_slot, low:high],
            send_sem=r_send.at[slot, piece], recv_sem=r_recv.at[to_slot, piece],
            device_id=(at_lat, wave), device_id_type=MESH)

    def pass_on(slot, job, e, from_sib, arrived, at_lat, to_slot):
        for piece, (low, high) in enumerate(PIECES):
            total = part[job, e, low:high] + sib[from_sib, low:high]
            for had in arrived:
                ring(0, piece, at_lat, had).wait_recv()
                total = total + rrcv[had, low:high].astype(F32)
            rsnd[slot, low:high] = total.astype(BF16)
            ring(slot, piece, at_lat, to_slot).start()

    one, two = 2 * up, 2 * chip_at(2)
    other = 1 - core

    def work(job, carry):
        toward = job % 2 == 0
        far = jnp.where(job == 0, 4, jnp.where(job == 7, 0, 3 - (job - 1) // 2))
        owner = chip_at(jnp.where(toward, far, -far))
        product(job, owner)

        @pl.when(job == 0)
        def _():
            to_sibling(0, other, 0).start()

        for k in (1, 3, 5):
            @pl.when(job == k)
            def _():
                to_sibling(k, 0, k).start()
                to_sibling(k, 1, k + 1).start()

        @pl.when(job == 7)
        def _():
            to_sibling(7, other, 7).start()

        @pl.when(job == 2)
        def _():
            to_sibling(0, other, 0).wait_recv()
            pass_on(0, 0, core, 0, (), two + core, 0)
            to_sibling(1, 0, 1).wait_recv()
            pass_on(1, 2, 0, 1, (), one + core, 1)
            to_sibling(1, 1, 2).wait_recv()
            pass_on(2, 2, 1, 2, (), one + core, 2)

        @pl.when(job == 6)
        def _():
            to_sibling(5, 0, 5).wait_recv()
            pass_on(3, 6, 0, 5, (), one, 3 + core)
            to_sibling(5, 1, 6).wait_recv()
            pass_on(4, 6, 1, 6, (), one + 1, 3 + core)

        @pl.when(job == 7)
        def _():
            to_sibling(3, 0, 3).wait_recv()
            to_sibling(3, 1, 4).wait_recv()
            pass_on(5 + other, 4, other, 3 + other, (1 + other,), two + other, 5 + core)
            pass_on(5 + core, 4, core, 3 + core, (1 + core, 0), two + core, 5 + core)

        return carry

    lax.fori_loop(0, 8, work, 0)

    to_sibling(7, other, 7).wait_recv()
    for slot in range(3, 7):
        for piece in range(len(PIECES)):
            ring(0, piece, one, slot).wait_recv()

    def total(low, high):
        return (part[7, core, low:high] + sib[7, low:high]
                + rrcv[3, low:high].astype(F32) + rrcv[4, low:high].astype(F32)
                + rrcv[5, low:high].astype(F32) + rrcv[6, low:high].astype(F32))

    t0, t1, t2, rest = total(0, 96), total(96, 192), total(192, 288), total(288, 304)
    spread = jnp.concatenate(
        [rest[8 * (c // 8):8 * (c // 8) + 8] if c % 8 == 0
         else pltpu.roll(rest[8 * (c // 8):8 * (c // 8) + 8], 128 - 16 * (c % 8), 1)
         for c in range(COLS)], axis=0)
    z = [t0,
         pltpu.roll(jnp.where(lane96 >= 80, t0, t1), 48, 1),
         pltpu.roll(t1, 96, 1),
         pltpu.roll(jnp.where(lane96 >= 112, t1, t2), 16, 1),
         pltpu.roll(jnp.where(lane96 >= 64, t2, spread), 64, 1)]
    degree = OWN * lat + lane8
    offset = jnp.where(degree < DEG // 2, 2 * degree, 2 * degree - (DEG - 1)).astype(F32)
    for q in range(GROUPS):
        inside = offset < lim[8 * q:8 * q + 8]
        for c in range(COLS):
            value = jnp.where(inside, z[q][8 * c:8 * c + 8], 0.0)
            out_ref[c, 8 * q:8 * q + 8, :] = value[:, :OWN]

    def sent(d, carry):
        exchange(d).wait_send()
        return carry

    lax.fori_loop(0, WAVES - 1, sent, 0)

    @pl.when(half == 1)
    def _():
        exchange(WAVES - 1).wait_send()

    for slot in range(8):
        to_sibling(0, 0, slot).wait_send()
    for slot in range(7):
        for piece in range(len(PIECES)):
            ring(slot, piece, one, 0).wait_send()


def local(fourier, wave_table, legendre):
    table = wave_table.reshape(10, 128)
    hbm = pl.BlockSpec(memory_space=pltpu.MemorySpace.HBM)
    out = pl.pallas_call(
        kernel,
        out_shape=jax.ShapeDtypeStruct((COLS, SLOTS, OWN), F32),
        in_specs=[hbm, hbm, hbm],
        out_specs=pl.BlockSpec(memory_space=pltpu.VMEM),
        scratch_shapes=[
            pltpu.VMEM((COLS, 2, DEG), BF16),
            pltpu.VMEM((10, 128), I32),
            pltpu.VMEM((SLOTS, PAIRS, DEG), BF16),
            pltpu.VMEM((3, 8, DEG), F32),
            pltpu.VMEM((33, 8, 128), BF16),
            pltpu.VMEM((32, 8, 128), BF16),
            pltpu.VMEM((2, 128, 128), F32),
            pltpu.VMEM((2, GROUPS, 96, 256), BF16),
            pltpu.VMEM((SLOTS, 128), F32),
            pltpu.VMEM((8, 2, ROWS, 128), F32),
            pltpu.VMEM((8, ROWS, 128), F32),
            pltpu.VMEM((7, ROWS, 128), BF16),
            pltpu.VMEM((7, ROWS, 128), BF16),
            pltpu.SemaphoreType.DMA((3,)),
            pltpu.SemaphoreType.DMA((WAVES,)),
            pltpu.SemaphoreType.DMA((WAVES,)),
            pltpu.SemaphoreType.DMA((8,)),
            pltpu.SemaphoreType.DMA((8,)),
            pltpu.SemaphoreType.DMA((7, len(PIECES))),
            pltpu.SemaphoreType.DMA((7, len(PIECES))),
        ],
        compiler_params=pltpu.CompilerParams(
            collective_id=0, has_side_effects=True, vmem_limit_bytes=52 << 20),
        name="legendre",
    )(jnp.transpose(fourier, (1, 0, 2)), table, legendre)
    return jnp.transpose(out, (1, 0, 2))


def solution(mesh):
    in_specs = (P(("lat", "wave"), None, None), P(), P("wave", "lat", None))
    out_specs = P("wave", None, "lat")
    return jax.shard_map(local, mesh=mesh, in_specs=in_specs, out_specs=out_specs, check_vma=False)
```

```python
import jax
import jax.numpy as jnp
from jax import lax
from jax.experimental import pallas as pl
from jax.experimental.pallas import tpu as pltpu
from jax.sharding import PartitionSpec as P

MESH = pl.DeviceIdType.MESH
F32, BF16, I32 = jnp.float32, jnp.bfloat16, jnp.int32

LATS, WAVES, CHIPS = 16, 32, 8
SLOTS, COLS, PAIRS, DEG = 40, 12, 32, 1280
OWN = 80
ROWS = 304
GROUPS = 5
PIECES = ((0, 160), (160, 304))


def lanes(shape):
    return lax.broadcasted_iota(I32, shape, len(shape) - 1)


def kernel(fo_hbm, wt_hbm, leg_hbm, out_ref, fo, wt, leg, vg, snd, ns, eo, lhs, lim,
           part, sib, rsnd, rrcv, in_sem, a_send, a_recv, s_send, s_recv, r_send, r_recv):
    lat = lax.axis_index("lat")
    wave = lax.axis_index("wave")
    chip, core = lat // 2, lat % 2
    step = 1 - 2 * core
    mirror = LATS - 1 - lat
    half = wave // 16
    target_lat = jnp.where(half == 1, mirror, lat)

    def chip_at(distance):
        return (chip + distance * step + 2 * CHIPS) % CHIPS

    up = chip_at(1)

    load_fo = pltpu.make_async_copy(fo_hbm, fo, in_sem.at[0])
    load_wt = pltpu.make_async_copy(wt_hbm, wt, in_sem.at[1])
    load_leg = pltpu.make_async_copy(leg_hbm, leg, in_sem.at[2])
    load_fo.start()
    load_wt.start()
    load_leg.start()

    barrier = pltpu.get_barrier_semaphore()

    def greet(d, carry):
        other = (wave + d) % WAVES
        at = jnp.where(other < 16, lat, mirror)
        pl.semaphore_signal(barrier, inc=1, device_id=(at, other), device_id_type=MESH)
        return carry

    lax.fori_loop(1, WAVES, greet, 0)

    @pl.when(half == 1)
    def _():
        pl.semaphore_signal(barrier, inc=1, device_id=(mirror, wave), device_id_type=MESH)

    pl.semaphore_signal(barrier, inc=1, device_id=(lat + step, wave), device_id_type=MESH)
    for away in (1, 2):
        for way in range(2):
            back = (chip + CHIPS - away * (1 - 2 * way)) % CHIPS
            pl.semaphore_signal(barrier, inc=1, device_id=(2 * back + way, wave), device_id_type=MESH)

    load_fo.wait()
    load_wt.wait()
    south = lat >= LATS // 2
    rows = fo[...].astype(F32)
    first, second = rows[:, 0, :], rows[:, 1, :]
    row_a = jnp.where(south, second, first)
    row_b = jnp.where(south, first, second)
    for g in range(3):
        vg[g] = jnp.concatenate([row_a[4 * g:4 * g + 4], row_b[4 * g:4 * g + 4]], axis=0)
    lane8 = lanes((8, 128))

    def table_lanes(start):
        row, off = start // 128, start % 128
        back = (128 - off) % 128
        near = jnp.broadcast_to(wt[pl.ds(row, 1), :], (8, 128))
        far = jnp.broadcast_to(wt[pl.ds(jnp.minimum(row + 1, 9), 1), :], (8, 128))
        return jnp.where(lane8 < 128 - off, pltpu.roll(near, back, 1), pltpu.roll(far, back, 1))

    def pick(t, carry):
        index = table_lanes(120 * t)
        low, high = index & 127, index >> 7
        found = []
        for g in range(3):
            acc = jnp.zeros((8, 128), F32)
            for u in range(10):
                got = jnp.take_along_axis(vg[g, :, 128 * u:128 * u + 128], low, axis=1,
                                          mode="promise_in_bounds")
                acc = jnp.where(high == u, got, acc)
            found.append(acc)
        for d in range(3):
            turned = [found[g] if g == d else pltpu.roll(found[g], (40 * (g - d)) % 128, 1)
                      for g in range(3)]
            message = jnp.where(lane8 < 40, turned[0], jnp.where(lane8 < 80, turned[1], turned[2]))
            snd[3 * t + d] = message.astype(BF16)
        return carry

    lax.fori_loop(0, 11, pick, 0, unroll=True)

    mine = jnp.broadcast_to(table_lanes(SLOTS * wave)[0:1].astype(F32), (128, 128))
    lim[...] = DEG - mine.T[:SLOTS]

    pl.semaphore_wait(barrier, 36 + half)

    place = jnp.where(south, 16 + 15 - wave % 16, wave % 16)

    def exchange(d):
        kz, kx = d // 4, d % 4
        dz = 4 + ((kz + 1) // 2) * (2 * (kz % 2) - 1) + 8
        dx = 2 + ((kx + 1) // 2) * (2 * (kx % 2) - 1) + 4
        to = 4 * ((wave // 4 + dz) % 8) + (wave + dx) % 4
        return pltpu.make_async_remote_copy(
            src_ref=snd.at[to], dst_ref=ns.at[place], send_sem=a_send.at[d],
            recv_sem=a_recv.at[place], device_id=(target_lat, to), device_id_type=MESH)

    def start_exchange(d, carry):
        exchange(d).start()
        return carry

    lax.fori_loop(0, WAVES - 1, start_exchange, 0)
    stay = pltpu.make_async_copy(snd.at[wave], ns.at[place], a_recv.at[place])

    @pl.when(half == 1)
    def _():
        exchange(WAVES - 1).start()

    @pl.when(half == 0)
    def _():
        stay.start()

    load_leg.wait()

    def arrive(s, carry):
        pltpu.make_async_copy(snd.at[0], ns.at[s], a_recv.at[s]).wait()
        return carry

    lax.fori_loop(0, WAVES, arrive, 0)

    north = ns[0:16].astype(F32)
    southern = ns[16:32].astype(F32)
    eo[0] = (north + southern).astype(BF16).astype(F32).reshape(128, 128)
    eo[1] = (north - southern).astype(BF16).astype(F32).reshape(128, 128)
    sub = lax.broadcasted_iota(I32, (8, 128), 0)
    keep = [sub == 4 * kt + lane8 // 32 for kt in range(2)]
    for part_of in range(2):
        for pair in range(2):
            turned = []
            for c4 in (2 * pair, 2 * pair + 1):
                x = eo[part_of, pl.ds(c4, 32, stride=4), :]
                turned.append(jnp.concatenate([x] * 4, axis=0).T)
            for g in range(3):
                c = 4 * g + 2 * pair
                for q in range(GROUPS):
                    at = 40 * g + 8 * q
                    for kt in range(2):
                        both = jnp.concatenate(
                            [jnp.where(keep[kt], t[at:at + 8], 0.0) for t in turned], axis=0)
                        lhs[part_of, q, 8 * c:8 * c + 16, 128 * kt:128 * kt + 128] = both.astype(BF16)

    lane96 = lanes((96, 128))

    def product(job, owner):
        off = 32 * (owner % 4)
        column = pl.multiple_of(128 * ((5 * owner) // 4), 128)
        placed = [[], []]
        for q in range(GROUPS):
            right = leg[8 * q:8 * q + 8, :, pl.ds(column, 256)].reshape(256, 256)
            got = jnp.dot(lhs[owner // 4, q], right, preferred_element_type=F32)
            for e in range(2):
                start = off + OWN * e
                window = jnp.where(lane96 >= start, got[:, :128], got[:, 128:])
                placed[e].append(pltpu.roll(window, (OWN * q + 256 - start) % 128, 1))
        for e in range(2):
            z = placed[e]
            part[job, e, 0:96] = jnp.where(lane96 < 80, z[0], z[1])
            part[job, e, 96:192] = jnp.where(lane96 < 32, z[1], jnp.where(lane96 < 112, z[2], z[3]))
            part[job, e, 192:288] = jnp.where(lane96 < 64, z[3], z[4])
            for v, count in ((0, 8), (1, 4)):
                rest = z[4][64 * v:64 * v + 8]
                for n in range(1, count):
                    c = 8 * v + n
                    rest = jnp.where(lane8 // 16 == n, pltpu.roll(z[4][8 * c:8 * c + 8], 16 * n, 1), rest)
                part[job, e, 288 + 8 * v:296 + 8 * v] = rest

    def to_sibling(job, e, slot):
        return pltpu.make_async_remote_copy(
            src_ref=part.at[job, e], dst_ref=sib.at[slot], send_sem=s_send.at[slot],
            recv_sem=s_recv.at[slot], device_id=(lat + step, wave), device_id_type=MESH)

    def ring(slot, piece, at_lat, to_slot):
        low, high = PIECES[piece]
        return pltpu.make_async_remote_copy(
            src_ref=rsnd.at[slot, low:high], dst_ref=rrcv.at[to_slot, low:high],
            send_sem=r_send.at[slot, piece], recv_sem=r_recv.at[to_slot, piece],
            device_id=(at_lat, wave), device_id_type=MESH)

    def pass_on(slot, job, e, from_sib, arrived, at_lat, to_slot):
        for piece, (low, high) in enumerate(PIECES):
            total = part[job, e, low:high] + sib[from_sib, low:high]
            for had in arrived:
                ring(0, piece, at_lat, had).wait_recv()
                total = total + rrcv[had, low:high].astype(F32)
            rsnd[slot, low:high] = total.astype(BF16)
            ring(slot, piece, at_lat, to_slot).start()

    one, two = 2 * up, 2 * chip_at(2)
    other = 1 - core

    def work(job, carry):
        toward = job % 2 == 0
        far = jnp.where(job == 0, 4, jnp.where(job == 7, 0, 3 - (job - 1) // 2))
        owner = chip_at(jnp.where(toward, far, -far))
        product(job, owner)

        @pl.when(job == 0)
        def _():
            to_sibling(0, other, 0).start()

        for k in (1, 3, 5):
            @pl.when(job == k)
            def _():
                to_sibling(k, 0, k).start()
                to_sibling(k, 1, k + 1).start()

        @pl.when(job == 7)
        def _():
            to_sibling(7, other, 7).start()

        @pl.when(job == 2)
        def _():
            to_sibling(0, other, 0).wait_recv()
            pass_on(0, 0, core, 0, (), two + core, 0)
            to_sibling(1, 0, 1).wait_recv()
            pass_on(1, 2, 0, 1, (), one + core, 1)
            to_sibling(1, 1, 2).wait_recv()
            pass_on(2, 2, 1, 2, (), one + core, 2)

        @pl.when(job == 6)
        def _():
            to_sibling(5, 0, 5).wait_recv()
            pass_on(3, 6, 0, 5, (), one, 3 + core)
            to_sibling(5, 1, 6).wait_recv()
            pass_on(4, 6, 1, 6, (), one + 1, 3 + core)

        @pl.when(job == 7)
        def _():
            to_sibling(3, 0, 3).wait_recv()
            to_sibling(3, 1, 4).wait_recv()
            pass_on(5 + other, 4, other, 3 + other, (1 + other,), two + other, 5 + core)
            pass_on(5 + core, 4, core, 3 + core, (1 + core, 0), two + core, 5 + core)

        return carry

    lax.fori_loop(0, 8, work, 0)

    to_sibling(7, other, 7).wait_recv()
    for slot in range(3, 7):
        for piece in range(len(PIECES)):
            ring(0, piece, one, slot).wait_recv()

    def total(low, high):
        return (part[7, core, low:high] + sib[7, low:high]
                + rrcv[3, low:high].astype(F32) + rrcv[4, low:high].astype(F32)
                + rrcv[5, low:high].astype(F32) + rrcv[6, low:high].astype(F32))

    t0, t1, t2, rest = total(0, 96), total(96, 192), total(192, 288), total(288, 304)
    spread = jnp.concatenate(
        [rest[8 * (c // 8):8 * (c // 8) + 8] if c % 8 == 0
         else pltpu.roll(rest[8 * (c // 8):8 * (c // 8) + 8], 128 - 16 * (c % 8), 1)
         for c in range(COLS)], axis=0)
    z = [t0,
         pltpu.roll(jnp.where(lane96 >= 80, t0, t1), 48, 1),
         pltpu.roll(t1, 96, 1),
         pltpu.roll(jnp.where(lane96 >= 112, t1, t2), 16, 1),
         pltpu.roll(jnp.where(lane96 >= 64, t2, spread), 64, 1)]
    degree = OWN * lat + lane8
    offset = jnp.where(degree < DEG // 2, 2 * degree, 2 * degree - (DEG - 1)).astype(F32)
    for q in range(GROUPS):
        inside = offset < lim[8 * q:8 * q + 8]
        for c in range(COLS):
            value = jnp.where(inside, z[q][8 * c:8 * c + 8], 0.0)
            out_ref[c, 8 * q:8 * q + 8, :] = value[:, :OWN]

    def sent(d, carry):
        exchange(d).wait_send()
        return carry

    lax.fori_loop(0, WAVES - 1, sent, 0)

    @pl.when(half == 1)
    def _():
        exchange(WAVES - 1).wait_send()

    for slot in range(8):
        to_sibling(0, 0, slot).wait_send()
    for slot in range(7):
        for piece in range(len(PIECES)):
            ring(slot, piece, one, 0).wait_send()


def local(fourier, wave_table, legendre):
    table = wave_table.reshape(10, 128)
    hbm = pl.BlockSpec(memory_space=pltpu.MemorySpace.HBM)
    out = pl.pallas_call(
        kernel,
        out_shape=jax.ShapeDtypeStruct((COLS, SLOTS, OWN), F32),
        in_specs=[hbm, hbm, hbm],
        out_specs=pl.BlockSpec(memory_space=pltpu.VMEM),
        scratch_shapes=[
            pltpu.VMEM((COLS, 2, DEG), BF16),
            pltpu.VMEM((10, 128), I32),
            pltpu.VMEM((SLOTS, PAIRS, DEG), BF16),
            pltpu.VMEM((3, 8, DEG), F32),
            pltpu.VMEM((33, 8, 128), BF16),
            pltpu.VMEM((32, 8, 128), BF16),
            pltpu.VMEM((2, 128, 128), F32),
            pltpu.VMEM((2, GROUPS, 96, 256), BF16),
            pltpu.VMEM((SLOTS, 128), F32),
            pltpu.VMEM((8, 2, ROWS, 128), F32),
            pltpu.VMEM((8, ROWS, 128), F32),
            pltpu.VMEM((7, ROWS, 128), BF16),
            pltpu.VMEM((7, ROWS, 128), BF16),
            pltpu.SemaphoreType.DMA((3,)),
            pltpu.SemaphoreType.DMA((WAVES,)),
            pltpu.SemaphoreType.DMA((WAVES,)),
            pltpu.SemaphoreType.DMA((8,)),
            pltpu.SemaphoreType.DMA((8,)),
            pltpu.SemaphoreType.DMA((7, len(PIECES))),
            pltpu.SemaphoreType.DMA((7, len(PIECES))),
        ],
        compiler_params=pltpu.CompilerParams(
            collective_id=0, has_side_effects=True, vmem_limit_bytes=52 << 20),
        name="legendre",
    )(*[pltpu.with_memory_space_constraint(a, pltpu.MemorySpace.HBM) for a in (jnp.transpose(fourier, (1, 0, 2)), table, legendre)])
    return jnp.transpose(out, (1, 0, 2))


def solution(mesh):
    in_specs = (P(("lat", "wave"), None, None), P(), P("wave", "lat", None))
    out_specs = P("wave", None, "lat")
    return jax.shard_map(local, mesh=mesh, in_specs=in_specs, out_specs=out_specs, check_vma=False)
```

```python
import jax
import jax.numpy as jnp
from jax import lax
from jax.experimental import pallas as pl
from jax.experimental.pallas import tpu as pltpu
from jax.sharding import PartitionSpec as P

MESH = pl.DeviceIdType.MESH
F32, BF16, I32 = jnp.float32, jnp.bfloat16, jnp.int32

LATS, WAVES, CHIPS = 16, 32, 8
SLOTS, COLS, PAIRS, DEG = 40, 12, 32, 1280
OWN = 80
ROWS = 304
GROUPS = 5
PIECES = ((0, 160), (160, 304))


def lanes(shape):
    return lax.broadcasted_iota(I32, shape, len(shape) - 1)


def kernel(fo_hbm, wt_hbm, leg_hbm, out_ref, fo, wt, leg, vg, snd, ns, eo, both, lhs, lim,
           part, rsnd, rrcv, in_sem, a_send, a_recv, x_send, x_recv, r_send, r_recv):
    lat = lax.axis_index("lat")
    wave = lax.axis_index("wave")
    chip, core = lat // 2, lat % 2
    step = 1 - 2 * core
    mirror = LATS - 1 - lat
    half = wave // 16
    target_lat = jnp.where(half == 1, mirror, lat)

    def chip_at(distance):
        return (chip + distance * step + 2 * CHIPS) % CHIPS

    up = chip_at(1)

    load_fo = pltpu.make_async_copy(fo_hbm, fo, in_sem.at[0])
    load_wt = pltpu.make_async_copy(wt_hbm, wt, in_sem.at[1])
    load_leg = pltpu.make_async_copy(leg_hbm, leg.at[0], in_sem.at[2])
    load_fo.start()
    load_wt.start()
    load_leg.start()

    barrier = pltpu.get_barrier_semaphore()

    def greet(d, carry):
        other = (wave + d) % WAVES
        at = jnp.where(other < 16, lat, mirror)
        pl.semaphore_signal(barrier, inc=1, device_id=(at, other), device_id_type=MESH)
        return carry

    lax.fori_loop(1, WAVES, greet, 0)

    @pl.when(half == 1)
    def _():
        pl.semaphore_signal(barrier, inc=1, device_id=(mirror, wave), device_id_type=MESH)

    pl.semaphore_signal(barrier, inc=1, device_id=(lat + step, wave), device_id_type=MESH)
    for away in (1, 2):
        for way in range(2):
            back = (chip + CHIPS - away * (1 - 2 * way)) % CHIPS
            pl.semaphore_signal(barrier, inc=1, device_id=(2 * back + way, wave), device_id_type=MESH)

    load_fo.wait()
    load_wt.wait()
    south = lat >= LATS // 2
    rows = fo[...].astype(F32)
    first, second = rows[:, 0, :], rows[:, 1, :]
    row_a = jnp.where(south, second, first)
    row_b = jnp.where(south, first, second)
    for g in range(3):
        vg[g] = jnp.concatenate([row_a[4 * g:4 * g + 4], row_b[4 * g:4 * g + 4]], axis=0)
    lane8 = lanes((8, 128))

    def table_lanes(start):
        row, off = start // 128, start % 128
        back = (128 - off) % 128
        near = jnp.broadcast_to(wt[pl.ds(row, 1), :], (8, 128))
        far = jnp.broadcast_to(wt[pl.ds(jnp.minimum(row + 1, 9), 1), :], (8, 128))
        return jnp.where(lane8 < 128 - off, pltpu.roll(near, back, 1), pltpu.roll(far, back, 1))

    def pick(t, carry):
        index = table_lanes(120 * t)
        low, high = index & 127, index >> 7
        found = []
        for g in range(3):
            acc = jnp.zeros((8, 128), F32)
            for u in range(10):
                got = jnp.take_along_axis(vg[g, :, 128 * u:128 * u + 128], low, axis=1,
                                          mode="promise_in_bounds")
                acc = jnp.where(high == u, got, acc)
            found.append(acc)
        for d in range(3):
            turned = [found[g] if g == d else pltpu.roll(found[g], (40 * (g - d)) % 128, 1)
                      for g in range(3)]
            message = jnp.where(lane8 < 40, turned[0], jnp.where(lane8 < 80, turned[1], turned[2]))
            snd[3 * t + d] = message.astype(BF16)
        return carry

    lax.fori_loop(0, 11, pick, 0, unroll=True)

    mine = jnp.broadcast_to(table_lanes(SLOTS * wave)[0:1].astype(F32), (128, 128))
    lim[...] = DEG - mine.T[:SLOTS]

    pl.semaphore_wait(barrier, 36 + half)

    place = jnp.where(south, 16 + 15 - wave % 16, wave % 16)

    def exchange(d):
        kz, kx = d // 4, d % 4
        dz = 4 + ((kz + 1) // 2) * (2 * (kz % 2) - 1) + 8
        dx = 2 + ((kx + 1) // 2) * (2 * (kx % 2) - 1) + 4
        to = 4 * ((wave // 4 + dz) % 8) + (wave + dx) % 4
        return pltpu.make_async_remote_copy(
            src_ref=snd.at[to], dst_ref=ns.at[place], send_sem=a_send.at[d],
            recv_sem=a_recv.at[place], device_id=(target_lat, to), device_id_type=MESH)

    def start_exchange(d, carry):
        exchange(d).start()
        return carry

    lax.fori_loop(0, WAVES - 1, start_exchange, 0)
    stay = pltpu.make_async_copy(snd.at[wave], ns.at[place], a_recv.at[place])

    @pl.when(half == 1)
    def _():
        exchange(WAVES - 1).start()

    @pl.when(half == 0)
    def _():
        stay.start()

    def to_sibling(src, dst, n):
        return pltpu.make_async_remote_copy(
            src_ref=src, dst_ref=dst, send_sem=x_send.at[n], recv_sem=x_recv.at[n],
            device_id=(lat + step, wave), device_id_type=MESH)

    give_leg = to_sibling(leg_hbm, leg.at[1], 0)
    give_leg.start()
    load_leg.wait()

    def arrive(s, carry):
        pltpu.make_async_copy(snd.at[0], ns.at[s], a_recv.at[s]).wait()
        return carry

    lax.fori_loop(0, WAVES, arrive, 0)

    north = ns[0:16].astype(F32)
    southern = ns[16:32].astype(F32)
    both[0, 0] = (north + southern).astype(BF16).reshape(128, 128)
    both[0, 1] = (north - southern).astype(BF16).reshape(128, 128)
    give_both = to_sibling(both.at[0], both.at[1], 1)
    give_both.start()
    sub = lax.broadcasted_iota(I32, (8, 128), 0)
    keep = [sub == 4 * kt + lane8 // 32 for kt in range(2)]

    def left_sides(source):
        eo[...] = both[source].astype(F32)
        for part_of in range(2):
            for pair in range(2):
                turned = []
                for c4 in (2 * pair, 2 * pair + 1):
                    x = eo[part_of, pl.ds(c4, 32, stride=4), :]
                    turned.append(jnp.concatenate([x] * 4, axis=0).T)
                for g in range(3):
                    c = 4 * g + 2 * pair
                    for q in range(GROUPS):
                        at = 40 * g + 8 * q
                        for kt in range(2):
                            two_c = jnp.concatenate(
                                [jnp.where(keep[kt], t[at:at + 8], 0.0) for t in turned], axis=0)
                            lhs[source, part_of, q, 8 * c:8 * c + 16,
                                128 * kt:128 * kt + 128] = two_c.astype(BF16)

    left_sides(0)
    give_both.wait_recv()
    left_sides(1)
    give_leg.wait_recv()

    lane96 = lanes((96, 128))

    def product(job, owner):
        off = 32 * (owner % 4)
        column = pl.multiple_of(128 * ((5 * owner) // 4), 128)
        placed = [[], []]
        for q in range(GROUPS):
            got = sum(
                jnp.dot(lhs[source, owner // 4, q],
                        leg[source, 8 * q:8 * q + 8, :, pl.ds(column, 256)].reshape(256, 256),
                        preferred_element_type=F32)
                for source in range(2))
            for e in range(2):
                start = off + OWN * e
                window = jnp.where(lane96 >= start, got[:, :128], got[:, 128:])
                placed[e].append(pltpu.roll(window, (OWN * q + 256 - start) % 128, 1))
        for e in range(2):
            z = placed[e]
            part[job, e, 0:96] = jnp.where(lane96 < 80, z[0], z[1])
            part[job, e, 96:192] = jnp.where(lane96 < 32, z[1], jnp.where(lane96 < 112, z[2], z[3]))
            part[job, e, 192:288] = jnp.where(lane96 < 64, z[3], z[4])
            for v, count in ((0, 8), (1, 4)):
                rest = z[4][64 * v:64 * v + 8]
                for n in range(1, count):
                    c = 8 * v + n
                    rest = jnp.where(lane8 // 16 == n, pltpu.roll(z[4][8 * c:8 * c + 8], 16 * n, 1), rest)
                part[job, e, 288 + 8 * v:296 + 8 * v] = rest

    def ring(slot, piece, at_lat, to_slot):
        low, high = PIECES[piece]
        return pltpu.make_async_remote_copy(
            src_ref=rsnd.at[slot, low:high], dst_ref=rrcv.at[to_slot, low:high],
            send_sem=r_send.at[slot, piece], recv_sem=r_recv.at[to_slot, piece],
            device_id=(at_lat, wave), device_id_type=MESH)

    def pass_on(slot, job, e, arrived, at_lat, to_slot):
        for piece, (low, high) in enumerate(PIECES):
            total = part[job, e, low:high]
            for had in arrived:
                ring(0, piece, at_lat, had).wait_recv()
                total = total + rrcv[had, low:high].astype(F32)
            rsnd[slot, low:high] = total.astype(BF16)
            ring(slot, piece, at_lat, to_slot).start()

    one, two = 2 * up, 2 * chip_at(2)
    other = 1 - core

    def work(job, carry):
        distance = jnp.where(job < 2, 3 + job, jnp.where(job < 4, job - 1, 0))
        product(job, chip_at(distance))

        @pl.when(job == 0)
        def _():
            pass_on(1 + other, 0, other, (), one + core, 1 + other)
            pass_on(1 + core, 0, core, (), one + core, 1 + core)

        @pl.when(job == 1)
        def _():
            pass_on(0, 1, core, (), two + core, 0)

        @pl.when(job == 2)
        def _():
            pass_on(3, 2, 0, (), one, 3 + core)
            pass_on(4, 2, 1, (), one + 1, 3 + core)

        @pl.when(job == 4)
        def _():
            pass_on(5 + other, 3, other, (1 + other,), two + other, 5 + core)
            pass_on(5 + core, 3, core, (1 + core, 0), two + core, 5 + core)

        return carry

    lax.fori_loop(0, 5, work, 0)

    for slot in range(3, 7):
        for piece in range(len(PIECES)):
            ring(0, piece, one, slot).wait_recv()

    def total(low, high):
        return (part[4, core, low:high]
                + rrcv[3, low:high].astype(F32) + rrcv[4, low:high].astype(F32)
                + rrcv[5, low:high].astype(F32) + rrcv[6, low:high].astype(F32))

    t0, t1, t2, rest = total(0, 96), total(96, 192), total(192, 288), total(288, 304)
    spread = jnp.concatenate(
        [rest[8 * (c // 8):8 * (c // 8) + 8] if c % 8 == 0
         else pltpu.roll(rest[8 * (c // 8):8 * (c // 8) + 8], 128 - 16 * (c % 8), 1)
         for c in range(COLS)], axis=0)
    z = [t0,
         pltpu.roll(jnp.where(lane96 >= 80, t0, t1), 48, 1),
         pltpu.roll(t1, 96, 1),
         pltpu.roll(jnp.where(lane96 >= 112, t1, t2), 16, 1),
         pltpu.roll(jnp.where(lane96 >= 64, t2, spread), 64, 1)]
    degree = OWN * lat + lane8
    offset = jnp.where(degree < DEG // 2, 2 * degree, 2 * degree - (DEG - 1)).astype(F32)
    for q in range(GROUPS):
        inside = offset < lim[8 * q:8 * q + 8]
        for c in range(COLS):
            value = jnp.where(inside, z[q][8 * c:8 * c + 8], 0.0)
            out_ref[c, 8 * q:8 * q + 8, :] = value[:, :OWN]

    def sent(d, carry):
        exchange(d).wait_send()
        return carry

    lax.fori_loop(0, WAVES - 1, sent, 0)

    @pl.when(half == 1)
    def _():
        exchange(WAVES - 1).wait_send()

    give_leg.wait_send()
    give_both.wait_send()
    for slot in range(7):
        for piece in range(len(PIECES)):
            ring(slot, piece, one, 0).wait_send()


def local(fourier, wave_table, legendre):
    table = wave_table.reshape(10, 128)
    hbm = pl.BlockSpec(memory_space=pltpu.MemorySpace.HBM)
    out = pl.pallas_call(
        kernel,
        out_shape=jax.ShapeDtypeStruct((COLS, SLOTS, OWN), F32),
        in_specs=[hbm, hbm, hbm],
        out_specs=pl.BlockSpec(memory_space=pltpu.VMEM),
        scratch_shapes=[
            pltpu.VMEM((COLS, 2, DEG), BF16),
            pltpu.VMEM((10, 128), I32),
            pltpu.VMEM((2, SLOTS, PAIRS, DEG), BF16),
            pltpu.VMEM((3, 8, DEG), F32),
            pltpu.VMEM((33, 8, 128), BF16),
            pltpu.VMEM((32, 8, 128), BF16),
            pltpu.VMEM((2, 128, 128), F32),
            pltpu.VMEM((2, 2, 128, 128), BF16),
            pltpu.VMEM((2, 2, GROUPS, 96, 256), BF16),
            pltpu.VMEM((SLOTS, 128), F32),
            pltpu.VMEM((5, 2, ROWS, 128), F32),
            pltpu.VMEM((7, ROWS, 128), BF16),
            pltpu.VMEM((7, ROWS, 128), BF16),
            pltpu.SemaphoreType.DMA((3,)),
            pltpu.SemaphoreType.DMA((WAVES,)),
            pltpu.SemaphoreType.DMA((WAVES,)),
            pltpu.SemaphoreType.DMA((2,)),
            pltpu.SemaphoreType.DMA((2,)),
            pltpu.SemaphoreType.DMA((7, len(PIECES))),
            pltpu.SemaphoreType.DMA((7, len(PIECES))),
        ],
        compiler_params=pltpu.CompilerParams(
            collective_id=0, has_side_effects=True, vmem_limit_bytes=52 << 20),
        name="legendre",
    )(*[pltpu.with_memory_space_constraint(a, pltpu.MemorySpace.HBM) for a in (jnp.transpose(fourier, (1, 0, 2)), table, legendre)])
    return jnp.transpose(out, (1, 0, 2))


def solution(mesh):
    in_specs = (P(("lat", "wave"), None, None), P(), P("wave", "lat", None))
    out_specs = P("wave", None, "lat")
    return jax.shard_map(local, mesh=mesh, in_specs=in_specs, out_specs=out_specs, check_vma=False)
```

```python
import jax
import jax.numpy as jnp
from jax import lax
from jax.experimental import pallas as pl
from jax.experimental.pallas import tpu as pltpu
from jax.sharding import PartitionSpec as P

MESH = pl.DeviceIdType.MESH
F32, BF16, I32 = jnp.float32, jnp.bfloat16, jnp.int32

LATS, WAVES, CHIPS = 16, 32, 8
SLOTS, COLS, PAIRS, DEG = 40, 12, 32, 1280
OWN = 80
ROWS = 304
GROUPS = 5
PIECES = ((0, 160), (160, 304))


def lanes(shape):
    return lax.broadcasted_iota(I32, shape, len(shape) - 1)


def kernel(fo_hbm, wt_hbm, leg_hbm, out_ref, fo, wt, leg, vg, snd, ns, eo, both, lhs, lim,
           part, rsnd, rrcv, in_sem, a_send, a_recv, x_send, x_recv, r_send, r_recv):
    lat = lax.axis_index("lat")
    wave = lax.axis_index("wave")
    chip, core = lat // 2, lat % 2
    step = 1 - 2 * core
    mirror = LATS - 1 - lat
    half = wave // 16
    target_lat = jnp.where(half == 1, mirror, lat)

    def chip_at(distance):
        return (chip + distance * step + 2 * CHIPS) % CHIPS

    up = chip_at(1)

    load_fo = pltpu.make_async_copy(fo_hbm, fo, in_sem.at[0])
    load_wt = pltpu.make_async_copy(wt_hbm, wt, in_sem.at[1])
    load_leg = pltpu.make_async_copy(leg_hbm, leg.at[0], in_sem.at[2])
    load_fo.start()
    load_wt.start()
    load_leg.start()

    barrier = pltpu.get_barrier_semaphore()

    def greet(d, carry):
        other = (wave + d) % WAVES
        at = jnp.where(other < 16, lat, mirror)
        pl.semaphore_signal(barrier, inc=1, device_id=(at, other), device_id_type=MESH)
        return carry

    lax.fori_loop(1, WAVES, greet, 0)

    @pl.when(half == 1)
    def _():
        pl.semaphore_signal(barrier, inc=1, device_id=(mirror, wave), device_id_type=MESH)

    pl.semaphore_signal(barrier, inc=1, device_id=(lat + step, wave), device_id_type=MESH)
    for away in (1, 2):
        for way in range(2):
            back = (chip + CHIPS - away * (1 - 2 * way)) % CHIPS
            pl.semaphore_signal(barrier, inc=1, device_id=(2 * back + way, wave), device_id_type=MESH)

    load_fo.wait()
    load_wt.wait()
    south = lat >= LATS // 2
    rows = fo[...].astype(F32)
    first, second = rows[:, 0, :], rows[:, 1, :]
    row_a = jnp.where(south, second, first)
    row_b = jnp.where(south, first, second)
    for g in range(3):
        vg[g] = jnp.concatenate([row_a[4 * g:4 * g + 4], row_b[4 * g:4 * g + 4]], axis=0)
    lane8 = lanes((8, 128))

    def table_lanes(start):
        row, off = start // 128, start % 128
        back = (128 - off) % 128
        near = jnp.broadcast_to(wt[pl.ds(row, 1), :], (8, 128))
        far = jnp.broadcast_to(wt[pl.ds(jnp.minimum(row + 1, 9), 1), :], (8, 128))
        return jnp.where(lane8 < 128 - off, pltpu.roll(near, back, 1), pltpu.roll(far, back, 1))

    def pick(t, carry):
        index = table_lanes(120 * t)
        low, high = index & 127, index >> 7
        found = []
        for g in range(3):
            acc = jnp.zeros((8, 128), F32)
            for u in range(10):
                got = jnp.take_along_axis(vg[g, :, 128 * u:128 * u + 128], low, axis=1,
                                          mode="promise_in_bounds")
                acc = jnp.where(high == u, got, acc)
            found.append(acc)
        for d in range(3):
            turned = [found[g] if g == d else pltpu.roll(found[g], (40 * (g - d)) % 128, 1)
                      for g in range(3)]
            message = jnp.where(lane8 < 40, turned[0], jnp.where(lane8 < 80, turned[1], turned[2]))
            snd[3 * t + d] = message.astype(BF16)
        return carry

    lax.fori_loop(0, 11, pick, 0, unroll=True)

    mine = jnp.broadcast_to(table_lanes(SLOTS * wave)[0:1].astype(F32), (128, 128))
    lim[...] = DEG - mine.T[:SLOTS]

    pl.semaphore_wait(barrier, 36 + half)

    place = jnp.where(south, 16 + 15 - wave % 16, wave % 16)

    def exchange(d):
        kz, kx = d // 4, d % 4
        dz = 4 + ((kz + 1) // 2) * (2 * (kz % 2) - 1) + 8
        dx = 2 + ((kx + 1) // 2) * (2 * (kx % 2) - 1) + 4
        to = 4 * ((wave // 4 + dz) % 8) + (wave + dx) % 4
        return pltpu.make_async_remote_copy(
            src_ref=snd.at[to], dst_ref=ns.at[place], send_sem=a_send.at[d],
            recv_sem=a_recv.at[place], device_id=(target_lat, to), device_id_type=MESH)

    def start_exchange(d, carry):
        exchange(d).start()
        return carry

    lax.fori_loop(0, WAVES - 1, start_exchange, 0)
    stay = pltpu.make_async_copy(snd.at[wave], ns.at[place], a_recv.at[place])

    @pl.when(half == 1)
    def _():
        exchange(WAVES - 1).start()

    @pl.when(half == 0)
    def _():
        stay.start()

    def to_sibling(src, dst, n):
        return pltpu.make_async_remote_copy(
            src_ref=src, dst_ref=dst, send_sem=x_send.at[n], recv_sem=x_recv.at[n],
            device_id=(lat + step, wave), device_id_type=MESH)

    give_leg = to_sibling(leg_hbm, leg.at[1], 0)
    give_leg.start()
    load_leg.wait()

    def arrive(s, carry):
        pltpu.make_async_copy(snd.at[0], ns.at[s], a_recv.at[s]).wait()
        return carry

    lax.fori_loop(0, WAVES, arrive, 0)

    north = ns[0:16].astype(F32)
    southern = ns[16:32].astype(F32)
    both[0, 0] = (north + southern).astype(BF16).reshape(128, 128)
    both[0, 1] = (north - southern).astype(BF16).reshape(128, 128)
    give_both = to_sibling(both.at[0], both.at[1], 1)
    give_both.start()
    sub = lax.broadcasted_iota(I32, (8, 128), 0)
    keep = [sub == 4 * kt + lane8 // 32 for kt in range(2)]

    def left_sides(source):
        eo[...] = both[source].astype(F32)
        for part_of in range(2):
            for pair in range(2):
                turned = []
                for c4 in (2 * pair, 2 * pair + 1):
                    x = eo[part_of, pl.ds(c4, 32, stride=4), :]
                    turned.append(jnp.concatenate([x] * 4, axis=0).T)
                for g in range(3):
                    c = 4 * g + 2 * pair
                    for q in range(GROUPS):
                        at = 40 * g + 8 * q
                        for kt in range(2):
                            two_c = jnp.concatenate(
                                [jnp.where(keep[kt], t[at:at + 8], 0.0) for t in turned], axis=0)
                            lhs[source, part_of, q, 8 * c:8 * c + 16,
                                128 * kt:128 * kt + 128] = two_c.astype(BF16)

    left_sides(0)
    give_both.wait_recv()
    left_sides(1)
    give_leg.wait_recv()

    lane96 = lanes((96, 128))

    def product(job, owner):
        off = 32 * (owner % 4)
        column = pl.multiple_of(128 * ((5 * owner) // 4), 128)
        placed = [[], []]
        for q in range(GROUPS):
            got = sum(
                jnp.dot(lhs[source, owner // 4, q],
                        leg[source, 8 * q:8 * q + 8, :, pl.ds(column, 256)].reshape(256, 256),
                        preferred_element_type=F32)
                for source in range(2))
            for e in range(2):
                start = off + OWN * e
                window = jnp.where(lane96 >= start, got[:, :128], got[:, 128:])
                placed[e].append(pltpu.roll(window, (OWN * q + 256 - start) % 128, 1))
        for e in range(2):
            z = placed[e]
            part[job, e, 0:96] = jnp.where(lane96 < 80, z[0], z[1])
            part[job, e, 96:192] = jnp.where(lane96 < 32, z[1], jnp.where(lane96 < 112, z[2], z[3]))
            part[job, e, 192:288] = jnp.where(lane96 < 64, z[3], z[4])
            for v, count in ((0, 8), (1, 4)):
                rest = z[4][64 * v:64 * v + 8]
                for n in range(1, count):
                    c = 8 * v + n
                    rest = jnp.where(lane8 // 16 == n, pltpu.roll(z[4][8 * c:8 * c + 8], 16 * n, 1), rest)
                part[job, e, 288 + 8 * v:296 + 8 * v] = rest

    def ring(slot, piece, at_lat, to_slot):
        low, high = PIECES[piece]
        return pltpu.make_async_remote_copy(
            src_ref=rsnd.at[slot, low:high], dst_ref=rrcv.at[to_slot, low:high],
            send_sem=r_send.at[slot, piece], recv_sem=r_recv.at[to_slot, piece],
            device_id=(at_lat, wave), device_id_type=MESH)

    def pass_on(slot, job, e, arrived, at_lat, to_slot):
        for piece, (low, high) in enumerate(PIECES):
            total = part[job, e, low:high]
            for had in arrived:
                ring(0, piece, at_lat, had).wait_recv()
                total = total + rrcv[had, low:high].astype(F32)
            rsnd[slot, low:high] = total.astype(BF16)
            ring(slot, piece, at_lat, to_slot).start()

    one, two = 2 * up, 2 * chip_at(2)
    other = 1 - core

    def work(job, carry):
        distance = jnp.where(job < 2, 4 - job, jnp.where(job < 4, job - 1, 0))
        product(job, chip_at(distance))

        @pl.when(job == 0)
        def _():
            pass_on(0, 0, core, (), two + core, 0)

        @pl.when(job == 1)
        def _():
            pass_on(1 + other, 1, other, (), one + core, 1 + other)
            pass_on(1 + core, 1, core, (), one + core, 1 + core)

        @pl.when(job == 2)
        def _():
            pass_on(3, 2, 0, (), one, 3 + core)
            pass_on(4, 2, 1, (), one + 1, 3 + core)

        @pl.when(job == 4)
        def _():
            pass_on(5 + other, 3, other, (1 + other,), two + other, 5 + core)
            pass_on(5 + core, 3, core, (1 + core, 0), two + core, 5 + core)

        return carry

    lax.fori_loop(0, 5, work, 0)

    def landed(slot):
        for piece in range(len(PIECES)):
            ring(0, piece, one, slot).wait_recv()

    landed(3)
    landed(4)
    part[4, core] += rrcv[3].astype(F32) + rrcv[4].astype(F32)
    landed(5)
    landed(6)

    def total(low, high):
        return (part[4, core, low:high]
                + rrcv[5, low:high].astype(F32) + rrcv[6, low:high].astype(F32))

    t0, t1, t2, rest = total(0, 96), total(96, 192), total(192, 288), total(288, 304)
    spread = jnp.concatenate(
        [rest[8 * (c // 8):8 * (c // 8) + 8] if c % 8 == 0
         else pltpu.roll(rest[8 * (c // 8):8 * (c // 8) + 8], 128 - 16 * (c % 8), 1)
         for c in range(COLS)], axis=0)
    z = [t0,
         pltpu.roll(jnp.where(lane96 >= 80, t0, t1), 48, 1),
         pltpu.roll(t1, 96, 1),
         pltpu.roll(jnp.where(lane96 >= 112, t1, t2), 16, 1),
         pltpu.roll(jnp.where(lane96 >= 64, t2, spread), 64, 1)]
    degree = OWN * lat + lane8
    offset = jnp.where(degree < DEG // 2, 2 * degree, 2 * degree - (DEG - 1)).astype(F32)
    for q in range(GROUPS):
        inside = offset < lim[8 * q:8 * q + 8]
        for c in range(COLS):
            value = jnp.where(inside, z[q][8 * c:8 * c + 8], 0.0)
            out_ref[c, 8 * q:8 * q + 8, :] = value[:, :OWN]

    def sent(d, carry):
        exchange(d).wait_send()
        return carry

    lax.fori_loop(0, WAVES - 1, sent, 0)

    @pl.when(half == 1)
    def _():
        exchange(WAVES - 1).wait_send()

    give_leg.wait_send()
    give_both.wait_send()
    for slot in range(7):
        for piece in range(len(PIECES)):
            ring(slot, piece, one, 0).wait_send()


def local(fourier, wave_table, legendre):
    table = wave_table.reshape(10, 128)
    hbm = pl.BlockSpec(memory_space=pltpu.MemorySpace.HBM)
    out = pl.pallas_call(
        kernel,
        out_shape=jax.ShapeDtypeStruct((COLS, SLOTS, OWN), F32),
        in_specs=[hbm, hbm, hbm],
        out_specs=pl.BlockSpec(memory_space=pltpu.VMEM),
        scratch_shapes=[
            pltpu.VMEM((COLS, 2, DEG), BF16),
            pltpu.VMEM((10, 128), I32),
            pltpu.VMEM((2, SLOTS, PAIRS, DEG), BF16),
            pltpu.VMEM((3, 8, DEG), F32),
            pltpu.VMEM((33, 8, 128), BF16),
            pltpu.VMEM((32, 8, 128), BF16),
            pltpu.VMEM((2, 128, 128), F32),
            pltpu.VMEM((2, 2, 128, 128), BF16),
            pltpu.VMEM((2, 2, GROUPS, 96, 256), BF16),
            pltpu.VMEM((SLOTS, 128), F32),
            pltpu.VMEM((5, 2, ROWS, 128), F32),
            pltpu.VMEM((7, ROWS, 128), BF16),
            pltpu.VMEM((7, ROWS, 128), BF16),
            pltpu.SemaphoreType.DMA((3,)),
            pltpu.SemaphoreType.DMA((WAVES,)),
            pltpu.SemaphoreType.DMA((WAVES,)),
            pltpu.SemaphoreType.DMA((2,)),
            pltpu.SemaphoreType.DMA((2,)),
            pltpu.SemaphoreType.DMA((7, len(PIECES))),
            pltpu.SemaphoreType.DMA((7, len(PIECES))),
        ],
        compiler_params=pltpu.CompilerParams(
            collective_id=0, has_side_effects=True, vmem_limit_bytes=52 << 20),
        name="legendre",
    )(*[pltpu.with_memory_space_constraint(a, pltpu.MemorySpace.HBM) for a in (jnp.transpose(fourier, (1, 0, 2)), table, legendre)])
    return jnp.transpose(out, (1, 0, 2))


def solution(mesh):
    in_specs = (P(("lat", "wave"), None, None), P(), P("wave", "lat", None))
    out_specs = P("wave", None, "lat")
    return jax.shard_map(local, mesh=mesh, in_specs=in_specs, out_specs=out_specs, check_vma=False)
```

```python
import jax
import jax.numpy as jnp
from jax import lax
from jax.experimental import pallas as pl
from jax.experimental.pallas import tpu as pltpu
from jax.sharding import PartitionSpec as P

MESH = pl.DeviceIdType.MESH
F32, BF16, I32 = jnp.float32, jnp.bfloat16, jnp.int32

LATS, WAVES, CHIPS = 16, 32, 8
SLOTS, COLS, PAIRS, DEG = 40, 12, 32, 1280
OWN = 80
ROWS = 304
GROUPS = 5
PIECES = ((0, 112), (112, 208), (208, 304))


def lanes(shape):
    return lax.broadcasted_iota(I32, shape, len(shape) - 1)


def kernel(fo_hbm, wt_hbm, leg_hbm, out_ref, fo, wt, leg, vg, snd, ns, eo, both, lhs, lim,
           part, rsnd, rrcv, in_sem, a_send, a_recv, x_send, x_recv, r_send, r_recv):
    lat = lax.axis_index("lat")
    wave = lax.axis_index("wave")
    chip, core = lat // 2, lat % 2
    step = 1 - 2 * core
    mirror = LATS - 1 - lat
    half = wave // 16
    target_lat = jnp.where(half == 1, mirror, lat)

    def chip_at(distance):
        return (chip + distance * step + 2 * CHIPS) % CHIPS

    up = chip_at(1)

    load_fo = pltpu.make_async_copy(fo_hbm, fo, in_sem.at[0])
    load_wt = pltpu.make_async_copy(wt_hbm, wt, in_sem.at[1])
    load_leg = pltpu.make_async_copy(leg_hbm, leg.at[0], in_sem.at[2])
    load_fo.start()
    load_wt.start()
    load_leg.start()

    barrier = pltpu.get_barrier_semaphore()

    def greet(d, carry):
        other = (wave + d) % WAVES
        at = jnp.where(other < 16, lat, mirror)
        pl.semaphore_signal(barrier, inc=1, device_id=(at, other), device_id_type=MESH)
        return carry

    lax.fori_loop(1, WAVES, greet, 0)

    @pl.when(half == 1)
    def _():
        pl.semaphore_signal(barrier, inc=1, device_id=(mirror, wave), device_id_type=MESH)

    pl.semaphore_signal(barrier, inc=1, device_id=(lat + step, wave), device_id_type=MESH)
    for away in (1, 2):
        for way in range(2):
            back = (chip + CHIPS - away * (1 - 2 * way)) % CHIPS
            pl.semaphore_signal(barrier, inc=1, device_id=(2 * back + way, wave), device_id_type=MESH)

    load_fo.wait()
    load_wt.wait()
    south = lat >= LATS // 2
    rows = fo[...].astype(F32)
    first, second = rows[:, 0, :], rows[:, 1, :]
    row_a = jnp.where(south, second, first)
    row_b = jnp.where(south, first, second)
    for g in range(3):
        vg[g] = jnp.concatenate([row_a[4 * g:4 * g + 4], row_b[4 * g:4 * g + 4]], axis=0)
    lane8 = lanes((8, 128))

    def table_lanes(start):
        row, off = start // 128, start % 128
        back = (128 - off) % 128
        near = jnp.broadcast_to(wt[pl.ds(row, 1), :], (8, 128))
        far = jnp.broadcast_to(wt[pl.ds(jnp.minimum(row + 1, 9), 1), :], (8, 128))
        return jnp.where(lane8 < 128 - off, pltpu.roll(near, back, 1), pltpu.roll(far, back, 1))

    def pick(t, carry):
        index = table_lanes(120 * t)
        low, high = index & 127, index >> 7
        found = []
        for g in range(3):
            acc = jnp.zeros((8, 128), F32)
            for u in range(10):
                got = jnp.take_along_axis(vg[g, :, 128 * u:128 * u + 128], low, axis=1,
                                          mode="promise_in_bounds")
                acc = jnp.where(high == u, got, acc)
            found.append(acc)
        for d in range(3):
            turned = [found[g] if g == d else pltpu.roll(found[g], (40 * (g - d)) % 128, 1)
                      for g in range(3)]
            message = jnp.where(lane8 < 40, turned[0], jnp.where(lane8 < 80, turned[1], turned[2]))
            snd[3 * t + d] = message.astype(BF16)
        return carry

    lax.fori_loop(0, 11, pick, 0, unroll=True)

    mine = jnp.broadcast_to(table_lanes(SLOTS * wave)[0:1].astype(F32), (128, 128))
    lim[...] = DEG - mine.T[:SLOTS]

    pl.semaphore_wait(barrier, 36 + half)

    place = jnp.where(south, 16 + 15 - wave % 16, wave % 16)

    def exchange(d):
        kz, kx = d // 4, d % 4
        dz = 4 + ((kz + 1) // 2) * (2 * (kz % 2) - 1) + 8
        dx = 2 + ((kx + 1) // 2) * (2 * (kx % 2) - 1) + 4
        to = 4 * ((wave // 4 + dz) % 8) + (wave + dx) % 4
        return pltpu.make_async_remote_copy(
            src_ref=snd.at[to], dst_ref=ns.at[place], send_sem=a_send.at[d],
            recv_sem=a_recv.at[place], device_id=(target_lat, to), device_id_type=MESH)

    def start_exchange(d, carry):
        exchange(d).start()
        return carry

    lax.fori_loop(0, WAVES - 1, start_exchange, 0)
    stay = pltpu.make_async_copy(snd.at[wave], ns.at[place], a_recv.at[place])

    @pl.when(half == 1)
    def _():
        exchange(WAVES - 1).start()

    @pl.when(half == 0)
    def _():
        stay.start()

    def to_sibling(src, dst, n):
        return pltpu.make_async_remote_copy(
            src_ref=src, dst_ref=dst, send_sem=x_send.at[n], recv_sem=x_recv.at[n],
            device_id=(lat + step, wave), device_id_type=MESH)

    give_leg = to_sibling(leg_hbm, leg.at[1], 0)
    give_leg.start()
    load_leg.wait()

    def arrive(s, carry):
        pltpu.make_async_copy(snd.at[0], ns.at[s], a_recv.at[s]).wait()
        return carry

    lax.fori_loop(0, WAVES, arrive, 0)

    north = ns[0:16].astype(F32)
    southern = ns[16:32].astype(F32)
    both[0, 0] = (north + southern).astype(BF16).reshape(128, 128)
    both[0, 1] = (north - southern).astype(BF16).reshape(128, 128)
    give_both = to_sibling(both.at[0], both.at[1], 1)
    give_both.start()
    sub = lax.broadcasted_iota(I32, (8, 128), 0)
    keep = [sub == 4 * kt + lane8 // 32 for kt in range(2)]

    def left_sides(source):
        eo[...] = both[source].astype(F32)
        for part_of in range(2):
            for pair in range(2):
                turned = []
                for c4 in (2 * pair, 2 * pair + 1):
                    x = eo[part_of, pl.ds(c4, 32, stride=4), :]
                    turned.append(jnp.concatenate([x] * 4, axis=0).T)
                for g in range(3):
                    c = 4 * g + 2 * pair
                    for q in range(GROUPS):
                        at = 40 * g + 8 * q
                        for kt in range(2):
                            two_c = jnp.concatenate(
                                [jnp.where(keep[kt], t[at:at + 8], 0.0) for t in turned], axis=0)
                            lhs[source, part_of, q, 8 * c:8 * c + 16,
                                128 * kt:128 * kt + 128] = two_c.astype(BF16)

    left_sides(0)
    give_both.wait_recv()
    left_sides(1)
    give_leg.wait_recv()

    lane96 = lanes((96, 128))

    def product(job, owner):
        off = 32 * (owner % 4)
        column = pl.multiple_of(128 * ((5 * owner) // 4), 128)
        placed = [[], []]
        for q in range(GROUPS):
            got = sum(
                jnp.dot(lhs[source, owner // 4, q],
                        leg[source, 8 * q:8 * q + 8, :, pl.ds(column, 256)].reshape(256, 256),
                        preferred_element_type=F32)
                for source in range(2))
            for e in range(2):
                start = off + OWN * e
                window = jnp.where(lane96 >= start, got[:, :128], got[:, 128:])
                placed[e].append(pltpu.roll(window, (OWN * q + 256 - start) % 128, 1))
        for e in range(2):
            z = placed[e]
            part[job, e, 0:96] = jnp.where(lane96 < 80, z[0], z[1])
            part[job, e, 96:192] = jnp.where(lane96 < 32, z[1], jnp.where(lane96 < 112, z[2], z[3]))
            part[job, e, 192:288] = jnp.where(lane96 < 64, z[3], z[4])
            for v, count in ((0, 8), (1, 4)):
                rest = z[4][64 * v:64 * v + 8]
                for n in range(1, count):
                    c = 8 * v + n
                    rest = jnp.where(lane8 // 16 == n, pltpu.roll(z[4][8 * c:8 * c + 8], 16 * n, 1), rest)
                part[job, e, 288 + 8 * v:296 + 8 * v] = rest

    def ring(slot, piece, at_lat, to_slot):
        low, high = PIECES[piece]
        return pltpu.make_async_remote_copy(
            src_ref=rsnd.at[slot, low:high], dst_ref=rrcv.at[to_slot, low:high],
            send_sem=r_send.at[slot, piece], recv_sem=r_recv.at[to_slot, piece],
            device_id=(at_lat, wave), device_id_type=MESH)

    def pass_on(slot, job, e, arrived, at_lat, to_slot):
        for piece, (low, high) in enumerate(PIECES):
            total = part[job, e, low:high]
            for had in arrived:
                ring(0, piece, at_lat, had).wait_recv()
                total = total + rrcv[had, low:high].astype(F32)
            rsnd[slot, low:high] = total.astype(BF16)
            ring(slot, piece, at_lat, to_slot).start()

    one, two = 2 * up, 2 * chip_at(2)
    other = 1 - core

    def work(job, carry):
        distance = jnp.where(job < 2, 4 - job, jnp.where(job < 4, job - 1, 0))
        product(job, chip_at(distance))

        @pl.when(job == 0)
        def _():
            pass_on(0, 0, core, (), two + core, 0)

        @pl.when(job == 1)
        def _():
            pass_on(1 + other, 1, other, (), one + core, 1 + other)
            pass_on(1 + core, 1, core, (), one + core, 1 + core)

        @pl.when(job == 2)
        def _():
            pass_on(3, 2, 0, (), one, 3 + core)
            pass_on(4, 2, 1, (), one + 1, 3 + core)

        @pl.when(job == 4)
        def _():
            pass_on(5 + other, 3, other, (1 + other,), two + other, 5 + core)
            pass_on(5 + core, 3, core, (1 + core, 0), two + core, 5 + core)

        return carry

    lax.fori_loop(0, 5, work, 0)

    def landed(slot):
        for piece in range(len(PIECES)):
            ring(0, piece, one, slot).wait_recv()

    landed(3)
    landed(4)
    part[4, core] += rrcv[3].astype(F32) + rrcv[4].astype(F32)
    landed(5)
    landed(6)

    def total(low, high):
        return (part[4, core, low:high]
                + rrcv[5, low:high].astype(F32) + rrcv[6, low:high].astype(F32))

    t0, t1, t2, rest = total(0, 96), total(96, 192), total(192, 288), total(288, 304)
    spread = jnp.concatenate(
        [rest[8 * (c // 8):8 * (c // 8) + 8] if c % 8 == 0
         else pltpu.roll(rest[8 * (c // 8):8 * (c // 8) + 8], 128 - 16 * (c % 8), 1)
         for c in range(COLS)], axis=0)
    z = [t0,
         pltpu.roll(jnp.where(lane96 >= 80, t0, t1), 48, 1),
         pltpu.roll(t1, 96, 1),
         pltpu.roll(jnp.where(lane96 >= 112, t1, t2), 16, 1),
         pltpu.roll(jnp.where(lane96 >= 64, t2, spread), 64, 1)]
    degree = OWN * lat + lane8
    offset = jnp.where(degree < DEG // 2, 2 * degree, 2 * degree - (DEG - 1)).astype(F32)
    for q in range(GROUPS):
        inside = offset < lim[8 * q:8 * q + 8]
        for c in range(COLS):
            value = jnp.where(inside, z[q][8 * c:8 * c + 8], 0.0)
            out_ref[c, 8 * q:8 * q + 8, :] = value[:, :OWN]

    def sent(d, carry):
        exchange(d).wait_send()
        return carry

    lax.fori_loop(0, WAVES - 1, sent, 0)

    @pl.when(half == 1)
    def _():
        exchange(WAVES - 1).wait_send()

    give_leg.wait_send()
    give_both.wait_send()
    for slot in range(7):
        for piece in range(len(PIECES)):
            ring(slot, piece, one, 0).wait_send()


def local(fourier, wave_table, legendre):
    table = wave_table.reshape(10, 128)
    hbm = pl.BlockSpec(memory_space=pltpu.MemorySpace.HBM)
    out = pl.pallas_call(
        kernel,
        out_shape=jax.ShapeDtypeStruct((COLS, SLOTS, OWN), F32),
        in_specs=[hbm, hbm, hbm],
        out_specs=pl.BlockSpec(memory_space=pltpu.VMEM),
        scratch_shapes=[
            pltpu.VMEM((COLS, 2, DEG), BF16),
            pltpu.VMEM((10, 128), I32),
            pltpu.VMEM((2, SLOTS, PAIRS, DEG), BF16),
            pltpu.VMEM((3, 8, DEG), F32),
            pltpu.VMEM((33, 8, 128), BF16),
            pltpu.VMEM((32, 8, 128), BF16),
            pltpu.VMEM((2, 128, 128), F32),
            pltpu.VMEM((2, 2, 128, 128), BF16),
            pltpu.VMEM((2, 2, GROUPS, 96, 256), BF16),
            pltpu.VMEM((SLOTS, 128), F32),
            pltpu.VMEM((5, 2, ROWS, 128), F32),
            pltpu.VMEM((7, ROWS, 128), BF16),
            pltpu.VMEM((7, ROWS, 128), BF16),
            pltpu.SemaphoreType.DMA((3,)),
            pltpu.SemaphoreType.DMA((WAVES,)),
            pltpu.SemaphoreType.DMA((WAVES,)),
            pltpu.SemaphoreType.DMA((2,)),
            pltpu.SemaphoreType.DMA((2,)),
            pltpu.SemaphoreType.DMA((7, len(PIECES))),
            pltpu.SemaphoreType.DMA((7, len(PIECES))),
        ],
        compiler_params=pltpu.CompilerParams(
            collective_id=0, has_side_effects=True, vmem_limit_bytes=52 << 20),
        name="legendre",
    )(*[pltpu.with_memory_space_constraint(a, pltpu.MemorySpace.HBM) for a in (jnp.transpose(fourier, (1, 0, 2)), table, legendre)])
    return jnp.transpose(out, (1, 0, 2))


def solution(mesh):
    in_specs = (P(("lat", "wave"), None, None), P(), P("wave", "lat", None))
    out_specs = P("wave", None, "lat")
    return jax.shard_map(local, mesh=mesh, in_specs=in_specs, out_specs=out_specs, check_vma=False)
```
